32 devices in a mesh: row: 4 (over y, x), col: 8 (over z, core).
Axes of the slice: x: 2, y: 2, z: 4, core: 2. Of those that a mesh axis runs over, the one named last changes fastest.
Arguments:
- features: bfloat16 [8192, 512], P(('col', 'row')), may hold values from -6 to 6
- order: int32 [8192], P('col'), may hold values from 0 to 8191, as said below
- tile_count: int32 [4, 8], P('row', 'col'), may hold values from 1 to 16, as said below
- tile_slots: int32 [4, 8, 16], P('row', 'col'), may hold values from 0 to 127, as said below
- blocks: bfloat16 [4, 8, 16, 128, 128], P('row', 'col'), may hold values from -0.3125 to 0.3125
- weight: bfloat16 [512, 512], replicated, may hold values from -0.25 to 0.25
Outputs:
- updated: bfloat16 [8192, 512], P(('row', 'col'))
The draws below stay inside these ranges and needn't reach their ends.
Inputs may be any that keep to these rules, and one draw needn't show every extreme that they name: order permutes each column group: positions j * 8 * 128 to (j + 1) * 8 * 128 - 1 name each node of that same range once. `tile_count`: some tile lists exactly 16 blocks in every draw. `tile_slots`: the codes of one tile's slots are distinct; slots at or beyond its count are unused.
All inputs are finite; a program needn't handle non-finite values.
Results may differ from the reference program's by a relative error of at most 0.01.
Values may be sent and summed in bfloat16 or wider, within the bound.
No kernel may reach another device: no remote copies, remote signals or barrier semaphores. Data moves between devices by JAX's collectives and lax.ppermute only.
A program may use at most 64 MiB of HBM per device.

```python
import jax
import jax.numpy as jnp
from jax import lax

F = 512
BLK = 128
CBLK = 8
RBLK = 16
TILE_MOST = 16
NODES = 8192
N_ROW = 4
N_COL = 8


def draw_order(key, part):
    group = CBLK * BLK
    groups = NODES // group
    keys = jax.random.split(key, groups)

    def shuffle(subkey):
        return jax.random.permutation(subkey, group)
    perms = jax.vmap(shuffle)(keys).astype(jnp.int32)
    offsets = (jnp.arange(groups, dtype=jnp.int32) * group)[:, None]
    return (perms + offsets).reshape(NODES)


def draw_tile_count(key, part):
    raw = jax.random.randint(jax.random.fold_in(key, 1), (N_ROW * N_COL,), 0, TILE_MOST)
    counts = 1 + raw * raw // TILE_MOST
    chosen = jax.random.randint(jax.random.fold_in(key, 2), (), 0, N_ROW * N_COL)
    counts = jnp.where(jnp.arange(N_ROW * N_COL) == chosen, TILE_MOST, counts)
    return counts.astype(jnp.int32).reshape(N_ROW, N_COL)


def draw_tile_slots(key, part):
    keys = jax.random.split(jax.random.fold_in(key, 3), N_ROW * N_COL)

    def shuffle(subkey):
        return jax.random.permutation(subkey, RBLK * CBLK)[:TILE_MOST]
    codes = jax.vmap(shuffle)(keys).astype(jnp.int32)
    return codes.reshape(N_ROW, N_COL, TILE_MOST)


def steps_of(stream_key, shape, pieces, smallest, largest):
    factor_of, own = 1.0, jax.random.fold_in(stream_key, 6)
    for position, parts in pieces:
        heights = jnp.exp(jax.random.uniform(jax.random.fold_in(own, position), (parts,), jnp.float32, smallest / len(pieces), largest / len(pieces)))
        factor_of = factor_of * jnp.repeat(heights, shape[position] // parts).reshape([-1 if axis == position else 1 for axis in range(len(shape))])
    return factor_of


def noise(stream_key, shape, spread, most, cuts=(), kind=jnp.bfloat16):
    entries = jax.random.normal(stream_key, shape, jnp.float32) * spread
    if len(cuts) > 0:
        entries = steps_of(stream_key, shape, cuts, -0.22, 0.18) * entries
    return jnp.clip(entries, min=-most, max=most).astype(kind)


def setup_inputs(seed: int = 0) -> dict:
    streams_of = jax.random.split(jax.random.key(seed), 7)
    features = noise(streams_of[0], (NODES, F), 1.0, 6.0, ((0, 32),))
    order = draw_order(jax.random.fold_in(streams_of[6], 71), 0)
    tile_count = draw_tile_count(jax.random.fold_in(streams_of[6], 71), 0)
    tile_slots = draw_tile_slots(jax.random.fold_in(streams_of[6], 71), 0)
    blocks = noise(streams_of[4], (N_ROW, N_COL, TILE_MOST, BLK, BLK), (N_COL * (TILE_MOST // 3 + 1) * BLK // RBLK) ** -0.5, 0.3125, ((0, 4), (1, 8)))
    weight = noise(streams_of[5], (F, F), F ** -0.5, 0.25)
    return {"features": features, "order": order, "tile_count": tile_count, "tile_slots": tile_slots, "blocks": blocks, "weight": weight}


def tile_partial(tile_blocks, codes, count, column_x):
    live = (jnp.arange(TILE_MOST) < count).astype(jnp.float32)
    block_row = codes // CBLK
    block_col = codes % CBLK
    xblocks = column_x.reshape(CBLK, BLK, F)[block_col].astype(jnp.float32)
    products = jnp.einsum("tab,tbf->taf", tile_blocks.astype(jnp.float32), xblocks)
    products = products * live[:, None, None]
    onehot = (block_row[:, None] == jnp.arange(RBLK)[None, :]).astype(jnp.float32)
    summed = jnp.einsum("tr,taf->raf", onehot, products)
    return summed.reshape(RBLK * BLK, F)


def reference(features, order, tile_count, tile_slots, blocks, weight):
    ordered = features[order]
    grouped = ordered.reshape(N_COL, CBLK * BLK, F)

    def one_row(row_index):
        def step(total, col_index):
            part = tile_partial(blocks[row_index, col_index], tile_slots[row_index, col_index],
                                tile_count[row_index, col_index], grouped[col_index])
            rounded = lax.optimization_barrier(part.astype(jnp.bfloat16))
            return total + rounded.astype(jnp.float32), None

        total, _ = lax.scan(step, jnp.zeros((RBLK * BLK, F), jnp.float32), jnp.arange(N_COL))
        return total

    aggregate = lax.map(one_row, jnp.arange(N_ROW)).reshape(NODES, F).astype(jnp.bfloat16)
    projected = jnp.dot(aggregate, weight, preferred_element_type=jnp.float32)
    return jax.nn.relu(projected).astype(jnp.bfloat16)
```

```python
import functools

import jax
import jax.numpy as jnp
from jax import lax
from jax.experimental import pallas as pl
from jax.experimental.pallas import tpu as pltpu
from jax.sharding import PartitionSpec as P

VMEM_LIMIT = 48 * 1024 * 1024
PARTS = 1


def chunk_slot(dest, here, chips):
    if chips != 4:
        return lax.rem(dest - here + chips, chips)
    even = lax.rem(here, 2) == 0
    first = jnp.where(even, 3, 0)
    second = lax.rem(here + 2, 4)
    return jnp.where(dest == here, 0, jnp.where(dest == second, 2, jnp.where(dest == first, 1, 3)))


def tile_kernel(chips, rows, shard, order_ref, count_ref, slots_ref, blocks_ref, keep_ref, give_ref):
    group = keep_ref.shape[1]
    width = blocks_ref.shape[-1]
    colblk = group // width
    piece = min(rows, width)
    me = lax.axis_index("col")
    row = lax.axis_index("row")
    chip, core = me // 2, lax.rem(me, 2)
    keep_ref[...] = jnp.zeros_like(keep_ref)
    give_ref[...] = jnp.zeros_like(give_ref)
    place = lax.broadcasted_iota(jnp.int32, (group, width), 0)
    corpus = ((place // shard) ^ row) * shard + place % shard + me * group

    def step(slot, carry):
        code = slots_ref[0, 0, slot]
        block_row = code // colblk
        block_col = lax.rem(code, colblk)
        nodes = order_ref[pl.ds(block_col, 1), :]
        onehot = jnp.where(corpus == nodes, 1.0, 0.0).astype(jnp.bfloat16)
        moved = lax.dot_general(
            blocks_ref[0, 0, slot], onehot, (((1,), (1,)), ((), ())),
            preferred_element_type=jnp.float32,
        ).astype(jnp.bfloat16)
        for part in range(width // piece):
            start = block_row * width + part * piece
            dest = start // rows
            at = chunk_slot(dest // 2, chip, chips) * rows + lax.rem(start, rows)
            at = pl.multiple_of(at, piece)
            values = moved[part * piece:(part + 1) * piece]

            @pl.when(lax.rem(dest, 2) == core)
            def _():
                keep_ref[pl.ds(at, piece), :] += values

            @pl.when(lax.rem(dest, 2) != core)
            def _():
                give_ref[pl.ds(at, piece), :] += values

        return carry

    lax.fori_loop(0, count_ref[0, 0], step, 0)


def sum_kernel(shards, own_tile_ref, other_tile_ref, *refs):
    features, outs = refs[:2 * shards], refs[2 * shards:]
    x = jnp.concatenate([ref[...] for ref in features[:shards]], axis=0)
    y = jnp.concatenate([ref[...] for ref in features[shards:]], axis=0)
    rows = outs[0].shape[0]
    for k, out in enumerate(outs):
        here = slice(k * rows, (k + 1) * rows)
        total = jnp.dot(own_tile_ref[here, :], x, preferred_element_type=jnp.float32)
        total += jnp.dot(other_tile_ref[here, :], y, preferred_element_type=jnp.float32)
        out[...] = total.astype(out.dtype)


def project_kernel(terms, *refs):
    ends_ref, weight_ref, out_ref = refs[-3], refs[-2], refs[-1]
    depth = refs[0].shape[1]
    projected = None
    for part in range((len(refs) - 3) // terms):
        mine = refs[part * terms:(part + 1) * terms]
        total = mine[0][...]
        for ref in mine[2:]:
            total += ref[...].astype(jnp.float32)
        first = mine[1][...].astype(jnp.float32)
        total += jnp.where(ends_ref[0] == 1, first, jnp.zeros_like(first))
        product = jnp.dot(
            total.astype(jnp.bfloat16), weight_ref[part * depth:(part + 1) * depth, :],
            preferred_element_type=jnp.float32,
        )
        projected = product if projected is None else projected + product
    out_ref[...] = jnp.maximum(projected, 0.0).astype(out_ref.dtype)


def over_chips(x, pairs):
    return lax.ppermute(x, "col", [(2 * a + c, 2 * b + c) for a, b in pairs for c in range(2)])


def per_device(features, order, tile_count, tile_slots, blocks, weight):
    rows_axis, cols_axis = lax.axis_size("row"), lax.axis_size("col")
    chips = cols_axis // 2
    shard, feats = features.shape
    group = shard * rows_axis
    width = blocks.shape[-1]
    rows = group // rows_axis
    params = pltpu.CompilerParams(vmem_limit_bytes=VMEM_LIMIT)
    smem = pl.BlockSpec(memory_space=pltpu.SMEM)
    vmem = pl.BlockSpec(memory_space=pltpu.VMEM)
    bf16 = jnp.bfloat16

    def other_core(x):
        return lax.ppermute(x, "col", [(j, j ^ 1) for j in range(cols_axis)])

    keep, give = pl.pallas_call(
        functools.partial(tile_kernel, chips, rows, shard),
        out_shape=[jax.ShapeDtypeStruct((chips * rows, group), bf16)] * 2,
        in_specs=[vmem, smem, smem, vmem],
        out_specs=[vmem, vmem],
        compiler_params=params,
    )(order.reshape(group // width, width), tile_count, tile_slots, blocks)
    other = other_core(give)

    depth = feats // PARTS
    chip = lax.axis_index("col") // 2
    ends = ((chip == 0) | (chip == chips - 1)) if chips == 4 else (chip >= 0)
    parts = []
    for part in range(PARTS):
        mine = features if PARTS == 1 else features[:, part * depth:(part + 1) * depth]
        gathered = [mine]
        for k in range(1, rows_axis):
            gathered.append(lax.ppermute(mine, "row", [(i, i ^ k) for i in range(rows_axis)]))
        swapped = [other_core(x) for x in gathered]
        sums = pl.pallas_call(
            functools.partial(sum_kernel, rows_axis),
            out_shape=[jax.ShapeDtypeStruct((rows, depth), jnp.float32)]
            + [jax.ShapeDtypeStruct((rows, depth), bf16)] * (chips - 1),
            in_specs=[vmem] * (2 + 2 * rows_axis),
            out_specs=[vmem] * chips,
            compiler_params=params,
        )(keep, other, *gathered, *swapped)
        if chips == 4:
            own, far, across, near = sums
            first = over_chips(far, [(0, 1), (1, 0), (2, 3), (3, 2)])
            inner = over_chips(near, [(1, 2), (2, 1)])
            added = jnp.where(ends, across, (across.astype(jnp.float32) + first.astype(jnp.float32)).astype(bf16))
            near, added = lax.optimization_barrier((near, added))
            outer = over_chips(near, [(0, 1), (3, 2)])
            last = over_chips(added, [(0, 2), (2, 0), (1, 3), (3, 1)])
            parts.append([own, first, inner, outer, last])
        else:
            received = [
                over_chips(sums[k], [(a, (a + k) % chips) for a in range(chips)])
                for k in range(1, chips)
            ]
            parts.append([sums[0], *received])
    terms = len(parts[0])
    return pl.pallas_call(
        functools.partial(project_kernel, terms),
        out_shape=jax.ShapeDtypeStruct((rows, feats), bf16),
        in_specs=[vmem] * (terms * PARTS) + [smem, vmem],
        out_specs=vmem,
        compiler_params=params,
    )(*[x for part in parts for x in part], ends.astype(jnp.int32).reshape(1), weight)


def solution(mesh):
    in_specs = (
        P(("col", "row"), None),
        P("col"),
        P("row", "col"),
        P("row", "col", None),
        P("row", "col", None, None, None),
        P(),
    )
    out_specs = P(("row", "col"), None)
    return jax.shard_map(
        per_device, mesh=mesh, in_specs=in_specs, out_specs=out_specs, check_vma=False
    )
```

```python
import functools

import jax
import jax.numpy as jnp
from jax import lax
from jax.experimental import pallas as pl
from jax.experimental.pallas import tpu as pltpu
from jax.sharding import PartitionSpec as P

VMEM_LIMIT = 16 * 1024 * 1024
SHARES = (1, 1)
COST = 10**10


def cut_kernel(x_hbm, *refs):
    outs, sems = refs[:-1], refs[-1]
    copies, start = [], 0
    for k, out in enumerate(outs):
        depth = out.shape[1]
        copies.append(pltpu.make_async_copy(x_hbm.at[:, pl.ds(start, depth)], out, sems.at[k]))
        start += depth
    for copy in copies:
        copy.start()
    for copy in copies:
        copy.wait()


def place_of(slot, bits):
    place = 0
    for bit in range(bits):
        place += ((slot >> (bit + 1)) & 1) << (bits - 1 - bit)
    return place


def tile_kernel(bits, rows, shard, order_hbm, blocks_hbm, count_ref, slots_ref, give_ref, keep_ref, pick_ref,
                order_ref, blocks_ref, sems):
    copies = [
        pltpu.make_async_copy(src, dst, sems.at[k])
        for k, (src, dst) in enumerate(((order_hbm, order_ref), (blocks_hbm, blocks_ref)))
    ]
    for copy in copies:
        copy.start()
    group = keep_ref.shape[1]
    width = blocks_ref.shape[-1]
    colblk = group // width
    piece = min(rows, width)
    me = lax.axis_index("col")
    row = lax.axis_index("row")
    keep_ref[...] = jnp.zeros_like(keep_ref)
    give_ref[...] = jnp.zeros_like(give_ref)
    place = lax.broadcasted_iota(jnp.int32, (width, group), 1)
    corpus = ((place // shard) ^ row) * shard + place % shard + me * group
    copies[0].wait()
    nodes = jnp.broadcast_to(order_ref[...][:, None, :], (colblk, width // colblk, width))
    nodes = nodes.reshape(width, width).T
    for k in range(colblk):
        column = nodes[:, k * (width // colblk):k * (width // colblk) + 1]
        pick_ref[k * width:(k + 1) * width, :] = jnp.where(corpus == column, 1.0, 0.0).astype(pick_ref.dtype)
    copies[1].wait()

    def step(index, carry):
        code = slots_ref[0, 0, index]
        columns = pl.ds(pl.multiple_of(lax.rem(code, colblk) * width, width), width)
        for part in range(width // piece):
            start = code // colblk * width + part * piece
            slot = (start // rows) ^ me
            at = place_of(slot, bits) * rows + lax.rem(start, rows)
            at = pl.ds(pl.multiple_of(at, piece), piece)
            values = blocks_ref[0, 0, index, part * piece:(part + 1) * piece, :]

            @pl.when(slot & 1 == 0)
            def _():
                keep_ref[at, columns] = values

            @pl.when(slot & 1 == 1)
            def _():
                give_ref[at, columns] = values

        return carry

    lax.fori_loop(0, count_ref[0, 0], step, 0)


def order_kernel(pick_ref, *refs):
    features, ordered_ref = refs[:-1], refs[-1]
    x = jnp.concatenate([ref[...] for ref in features], axis=0)
    ordered_ref[...] = jnp.dot(pick_ref[...], x, preferred_element_type=jnp.float32).astype(ordered_ref.dtype)


def sum_kernel(tile_ref, ordered_ref, out_ref):
    out_ref[...] = jnp.dot(tile_ref[...], ordered_ref[...], preferred_element_type=jnp.float32).astype(out_ref.dtype)


def add_kernel(mine_ref, got_ref, hold_ref, *sends):
    count = hold_ref.shape[0]
    hold_ref[...] = mine_ref[:count, :] + got_ref[:count, :].astype(jnp.float32)
    for send_ref in sends:
        here = slice(count, count + send_ref.shape[0])
        send_ref[...] = (mine_ref[here, :] + got_ref[here, :].astype(jnp.float32)).astype(send_ref.dtype)
        count += send_ref.shape[0]


def relay_kernel(mine_ref, got_ref, *sends):
    offset = got_ref.shape[0]
    start = 0
    for send_ref in sends:
        count = send_ref.shape[0]
        total = mine_ref[offset + start:offset + start + count, :] + got_ref[start:start + count, :].astype(jnp.float32)
        send_ref[...] = total.astype(send_ref.dtype)
        start += count


def keep_kernel(mine_ref, got_ref, hold_ref):
    hold_ref[...] = mine_ref[:hold_ref.shape[0], :] + got_ref[...].astype(jnp.float32)


def project_kernel(*refs):
    weight_ref, out_ref = refs[-2], refs[-1]
    projected, start = None, 0
    for part in range((len(refs) - 2) // 3):
        mine_ref, near_ref, far_ref = refs[3 * part:3 * part + 3]
        total = mine_ref[:near_ref.shape[0], :] + near_ref[...].astype(jnp.float32) + far_ref[...].astype(jnp.float32)
        depth = total.shape[1]
        product = jnp.dot(
            total.astype(jnp.bfloat16), weight_ref[start:start + depth, :], preferred_element_type=jnp.float32
        )
        projected = product if projected is None else projected + product
        start += depth
    out_ref[...] = jnp.maximum(projected, 0.0).astype(out_ref.dtype)


def per_device(features, order, tile_count, tile_slots, blocks, weight):
    rows_axis, cols_axis = lax.axis_size("row"), lax.axis_size("col")
    bits = cols_axis.bit_length() - 2
    half = cols_axis // 2
    shard, feats = features.shape
    group = shard * rows_axis
    width = blocks.shape[-1]
    rows = shard
    params = pltpu.CompilerParams(vmem_limit_bytes=VMEM_LIMIT)
    vmem = pl.BlockSpec(memory_space=pltpu.VMEM)
    smem = pl.BlockSpec(memory_space=pltpu.SMEM)
    hbm = pl.BlockSpec(memory_space=pltpu.HBM)
    bf16, f32 = jnp.bfloat16, jnp.float32
    shape = jax.ShapeDtypeStruct

    def call(kernel, outs, ins, specs=None, scratch=(), cost=COST):
        return pl.pallas_call(
            kernel,
            out_shape=outs,
            in_specs=specs or [vmem] * len(ins),
            out_specs=jax.tree.map(lambda _: vmem, outs),
            scratch_shapes=scratch,
            compiler_params=params,
            cost_estimate=pl.CostEstimate(flops=cost, bytes_accessed=cost, transcendentals=0),
        )(*ins)

    def in_hbm(x):
        return pltpu.with_memory_space_constraint(x, pltpu.HBM)

    def after(x, *done):
        return lax.optimization_barrier((x, *done))[0]

    def exchange(x, axis, distance):
        return lax.ppermute(x, axis, [(i, i ^ distance) for i in range(lax.axis_size(axis))])

    widths = [feats * share // sum(SHARES) for share in SHARES]
    cuts = call(
        cut_kernel, [shape((shard, depth), bf16) for depth in widths], [in_hbm(features)],
        [hbm], [pltpu.SemaphoreType.DMA((len(widths),))], 1,
    )
    gathered = [[mine] + [exchange(mine, "row", k) for k in range(1, rows_axis)] for mine in cuts]
    table = (group // width, width)
    give, keep, pick = call(
        functools.partial(tile_kernel, bits, rows, shard),
        [shape((half * rows, group), bf16)] * 2 + [shape((group, group), bf16)],
        [in_hbm(order.reshape(table)), in_hbm(blocks), tile_count, tile_slots],
        [hbm, hbm, smem, smem],
        [
            pltpu.VMEM(table, jnp.int32),
            pltpu.VMEM(blocks.shape, bf16),
            pltpu.SemaphoreType.DMA((2,)),
        ],
    )

    def pieces(count, depth):
        return [shape((count // 2 * rows, depth), bf16)] * 2 if count > 1 else [shape((rows, depth), bf16)]

    def first_step(mine, got, *done):
        depth = mine.shape[1]
        outs = [shape((half // 2 * rows, depth), f32)] + pieces(half // 2, depth)
        hold, low, high = call(add_kernel, outs, [mine, got])
        if done:
            high = after(high, *done)
        return hold, exchange(high, "col", 2), exchange(low, "col", 2)

    def later_steps(hold, high, low):
        distance, depth = 4, hold.shape[1]
        while True:
            count = hold.shape[0] // (2 * rows)
            sends = call(relay_kernel, pieces(count, depth), [hold, high])
            sent[:] = sends
            if count == 1:
                return [hold, low, exchange(sends[0], "col", distance)]
            hold = call(keep_kernel, shape((count * rows, depth), f32), [hold, low])
            low, high = [exchange(send, "col", distance) for send in sends]
            distance *= 2

    ends, waiting, sent = [], None, []
    for features, depth in zip(gathered, widths, strict=True):
        if waiting is not None:
            features = [after(features[0], waiting[0]), *features[1:]]
        ordered = call(order_kernel, shape((group, depth), bf16), [pick, *features])
        given = call(sum_kernel, shape((half * rows, depth), bf16), [give, ordered])
        got = exchange(given, "col", 1)
        if waiting is not None:
            ends += later_steps(waiting[0], after(waiting[1], given), waiting[2])
            ordered = after(ordered, sent[0])
        mine = call(sum_kernel, shape((half * rows, depth), f32), [keep, ordered])
        waiting = first_step(mine, got, *([] if waiting is None else [waiting[2]]))
    ends += later_steps(*waiting)
    return call(project_kernel, shape((rows, feats), bf16), [*ends, weight])


def solution(mesh):
    in_specs = (
        P(("col", "row"), None),
        P("col"),
        P("row", "col"),
        P("row", "col", None),
        P("row", "col", None, None, None),
        P(),
    )
    out_specs = P(("row", "col"), None)
    return jax.shard_map(
        per_device, mesh=mesh, in_specs=in_specs, out_specs=out_specs, check_vma=False
    )
```

```python
import functools

import jax
import jax.numpy as jnp
from jax import lax
from jax.experimental import pallas as pl
from jax.experimental.pallas import tpu as pltpu
from jax.sharding import PartitionSpec as P

VMEM_LIMIT = 16 * 1024 * 1024
SHARES = (1, 1)
COST = 10**10


def cut_kernel(x_hbm, *refs):
    outs, sems = refs[:-1], refs[-1]
    copies, start = [], 0
    for k, out in enumerate(outs):
        depth = out.shape[1]
        copies.append(pltpu.make_async_copy(x_hbm.at[:, pl.ds(start, depth)], out, sems.at[k]))
        start += depth
    for copy in copies:
        copy.start()
    for copy in copies:
        copy.wait()


def place_of(slot, core, bits):
    near = 0
    for bit in range(bits):
        near += ((slot >> (bit + 1)) & 1) << (bits - 1 - bit)
    return jnp.where(core == 0, near, slot >> 1)


def tile_kernel(bits, rows, shard, order_hbm, blocks_hbm, count_ref, slots_ref, give_ref, keep_ref, pick_ref,
                order_ref, blocks_ref, sems):
    copies = [
        pltpu.make_async_copy(src, dst, sems.at[k])
        for k, (src, dst) in enumerate(((order_hbm, order_ref), (blocks_hbm, blocks_ref)))
    ]
    for copy in copies:
        copy.start()
    group = keep_ref.shape[1]
    width = blocks_ref.shape[-1]
    colblk = group // width
    piece = min(rows, width)
    me = lax.axis_index("col")
    row = lax.axis_index("row")
    keep_ref[...] = jnp.zeros_like(keep_ref)
    give_ref[...] = jnp.zeros_like(give_ref)
    place = lax.broadcasted_iota(jnp.int32, (width, group), 1)
    corpus = ((place // shard) ^ row) * shard + place % shard + me * group
    copies[0].wait()
    nodes = jnp.broadcast_to(order_ref[...][:, None, :], (colblk, width // colblk, width))
    nodes = nodes.reshape(width, width).T
    for k in range(colblk):
        column = nodes[:, k * (width // colblk):k * (width // colblk) + 1]
        pick_ref[k * width:(k + 1) * width, :] = jnp.where(corpus == column, 1.0, 0.0).astype(pick_ref.dtype)
    copies[1].wait()

    def step(index, carry):
        code = slots_ref[0, 0, index]
        columns = pl.ds(pl.multiple_of(lax.rem(code, colblk) * width, width), width)
        for part in range(width // piece):
            start = code // colblk * width + part * piece
            slot = (start // rows) ^ me
            at = place_of(slot, (me ^ slot) & 1, bits) * rows + lax.rem(start, rows)
            at = pl.ds(pl.multiple_of(at, piece), piece)
            values = blocks_ref[0, 0, index, part * piece:(part + 1) * piece, :]

            @pl.when(slot & 1 == 0)
            def _():
                keep_ref[at, columns] = values

            @pl.when(slot & 1 == 1)
            def _():
                give_ref[at, columns] = values

        return carry

    lax.fori_loop(0, count_ref[0, 0], step, 0)


def order_kernel(pick_ref, *refs):
    features, ordered_ref = refs[:-1], refs[-1]
    x = jnp.concatenate([ref[...] for ref in features], axis=0)
    ordered_ref[...] = jnp.dot(pick_ref[...], x, preferred_element_type=jnp.float32).astype(ordered_ref.dtype)


def sum_kernel(tile_ref, ordered_ref, out_ref):
    out_ref[...] = jnp.dot(tile_ref[...], ordered_ref[...], preferred_element_type=jnp.float32).astype(out_ref.dtype)


def add_kernel(mine_ref, got_ref, hold_ref, *sends):
    count = hold_ref.shape[0]
    hold_ref[...] = mine_ref[:count, :] + got_ref[:count, :].astype(jnp.float32)
    for send_ref in sends:
        here = slice(count, count + send_ref.shape[0])
        send_ref[...] = (mine_ref[here, :] + got_ref[here, :].astype(jnp.float32)).astype(send_ref.dtype)
        count += send_ref.shape[0]


def relay_kernel(mine_ref, got_ref, *sends):
    offset = got_ref.shape[0]
    start = 0
    for send_ref in sends:
        count = send_ref.shape[0]
        total = mine_ref[offset + start:offset + start + count, :] + got_ref[start:start + count, :].astype(jnp.float32)
        send_ref[...] = total.astype(send_ref.dtype)
        start += count


def keep_kernel(mine_ref, got_ref, hold_ref):
    hold_ref[...] = mine_ref[:hold_ref.shape[0], :] + got_ref[...].astype(jnp.float32)


def project_kernel(*refs):
    weight_ref, out_ref = refs[-2], refs[-1]
    projected, start = None, 0
    for part in range((len(refs) - 2) // 3):
        mine_ref, near_ref, far_ref = refs[3 * part:3 * part + 3]
        total = mine_ref[:near_ref.shape[0], :] + near_ref[...].astype(jnp.float32) + far_ref[...].astype(jnp.float32)
        depth = total.shape[1]
        product = jnp.dot(
            total.astype(jnp.bfloat16), weight_ref[start:start + depth, :], preferred_element_type=jnp.float32
        )
        projected = product if projected is None else projected + product
        start += depth
    out_ref[...] = jnp.maximum(projected, 0.0).astype(out_ref.dtype)


def per_device(features, order, tile_count, tile_slots, blocks, weight):
    rows_axis, cols_axis = lax.axis_size("row"), lax.axis_size("col")
    bits = cols_axis.bit_length() - 2
    half = cols_axis // 2
    shard, feats = features.shape
    group = shard * rows_axis
    width = blocks.shape[-1]
    rows = shard
    params = pltpu.CompilerParams(vmem_limit_bytes=VMEM_LIMIT)
    vmem = pl.BlockSpec(memory_space=pltpu.VMEM)
    smem = pl.BlockSpec(memory_space=pltpu.SMEM)
    hbm = pl.BlockSpec(memory_space=pltpu.HBM)
    bf16, f32 = jnp.bfloat16, jnp.float32
    shape = jax.ShapeDtypeStruct

    def call(kernel, outs, ins, specs=None, scratch=(), cost=COST):
        return pl.pallas_call(
            kernel,
            out_shape=outs,
            in_specs=specs or [vmem] * len(ins),
            out_specs=jax.tree.map(lambda _: vmem, outs),
            scratch_shapes=scratch,
            compiler_params=params,
            cost_estimate=pl.CostEstimate(flops=cost, bytes_accessed=cost, transcendentals=0),
        )(*ins)

    def in_hbm(x):
        return pltpu.with_memory_space_constraint(x, pltpu.HBM)

    def after(x, *done):
        return lax.optimization_barrier((x, *done))[0]

    def exchange(x, axis, distance):
        return lax.ppermute(x, axis, [(i, i ^ distance) for i in range(lax.axis_size(axis))])

    def exchange_chips(x, step):
        far = cols_axis >> (step + 1)
        near = 2 << step
        return lax.ppermute(x, "col", [(j, j ^ (far if j & 1 else near)) for j in range(cols_axis)])

    widths = [feats * share // sum(SHARES) for share in SHARES]
    cuts = call(
        cut_kernel, [shape((shard, depth), bf16) for depth in widths], [in_hbm(features)],
        [hbm], [pltpu.SemaphoreType.DMA((len(widths),))], 1,
    )
    gathered = [[mine] + [exchange(mine, "row", k) for k in range(1, rows_axis)] for mine in cuts]
    table = (group // width, width)
    give, keep, pick = call(
        functools.partial(tile_kernel, bits, rows, shard),
        [shape((half * rows, group), bf16)] * 2 + [shape((group, group), bf16)],
        [in_hbm(order.reshape(table)), in_hbm(blocks), tile_count, tile_slots],
        [hbm, hbm, smem, smem],
        [
            pltpu.VMEM(table, jnp.int32),
            pltpu.VMEM(blocks.shape, bf16),
            pltpu.SemaphoreType.DMA((2,)),
        ],
    )

    def pieces(count, depth):
        return [shape((count // 2 * rows, depth), bf16)] * 2 if count > 1 else [shape((rows, depth), bf16)]

    def first_step(mine, got):
        depth = mine.shape[1]
        outs = [shape((half // 2 * rows, depth), f32)] + pieces(half // 2, depth)
        hold, low, high = call(add_kernel, outs, [mine, got])
        return hold, exchange_chips(high, 0), exchange_chips(low, 0)

    def later_steps(hold, high, low):
        step, depth = 1, hold.shape[1]
        while True:
            count = hold.shape[0] // (2 * rows)
            sends = call(relay_kernel, pieces(count, depth), [hold, high])
            sent[:] = sends
            if count == 1:
                return [hold, low, exchange_chips(sends[0], step)]
            hold = call(keep_kernel, shape((count * rows, depth), f32), [hold, low])
            low, high = [exchange_chips(send, step) for send in sends]
            step += 1

    ends, waiting, sent, lows = [], None, [], []
    for features, depth in zip(gathered, widths, strict=True):
        if waiting is not None:
            features = [after(features[0], waiting[0]), *features[1:]]
        ordered = call(order_kernel, shape((group, depth), bf16), [pick, *features])
        given = call(sum_kernel, shape((half * rows, depth), bf16), [give, ordered])
        got = exchange(given, "col", 1)
        if waiting is not None:
            ends += later_steps(waiting[0], after(waiting[1], given), waiting[2])
            ordered = after(ordered, sent[0])
        mine = call(sum_kernel, shape((half * rows, depth), f32), [keep, ordered])
        waiting = first_step(mine, got)
        lows.append(waiting[2])
    ends += later_steps(waiting[0], after(waiting[1], *lows[:-1], *ends[2::3]), waiting[2])
    return call(project_kernel, shape((rows, feats), bf16), [*ends, weight])


def solution(mesh):
    in_specs = (
        P(("col", "row"), None),
        P("col"),
        P("row", "col"),
        P("row", "col", None),
        P("row", "col", None, None, None),
        P(),
    )
    out_specs = P(("row", "col"), None)
    return jax.shard_map(
        per_device, mesh=mesh, in_specs=in_specs, out_specs=out_specs, check_vma=False
    )
```

```python
import functools

import jax
import jax.numpy as jnp
from jax import lax
from jax.experimental import pallas as pl
from jax.experimental.pallas import tpu as pltpu
from jax.sharding import PartitionSpec as P

VMEM_LIMIT = 16 * 1024 * 1024
SHARES = (1, 1)
COST = 10**10


def cut_kernel(x_hbm, *refs):
    outs, sems = refs[:-1], refs[-1]
    copies, start = [], 0
    for k, out in enumerate(outs):
        depth = out.shape[1]
        copies.append(pltpu.make_async_copy(x_hbm.at[:, pl.ds(start, depth)], out, sems.at[k]))
        start += depth
    for copy in copies:
        copy.start()
    for copy in copies:
        copy.wait()


def place_of(slot, core, bits):
    near = 0
    for bit in range(bits):
        near += ((slot >> (bit + 1)) & 1) << (bits - 1 - bit)
    return jnp.where(core == 0, near, slot >> 1)


def tile_kernel(bits, rows, shard, order_hbm, blocks_hbm, slots_hbm, count_ref, give_ref, keep_ref, pick_ref,
                order_ref, blocks_ref, slots_ref, sems):
    copies = [
        pltpu.make_async_copy(src, dst, sems.at[k])
        for k, (src, dst) in enumerate(((order_hbm, order_ref), (blocks_hbm, blocks_ref), (slots_hbm, slots_ref)))
    ]
    for copy in copies:
        copy.start()
    group = keep_ref.shape[1]
    width = blocks_ref.shape[-1]
    colblk = group // width
    piece = min(rows, width)
    me = lax.axis_index("col")
    row = lax.axis_index("row")
    keep_ref[...] = jnp.zeros_like(keep_ref)
    give_ref[...] = jnp.zeros_like(give_ref)
    place = lax.broadcasted_iota(jnp.int32, (width, group), 1)
    corpus = ((place // shard) ^ row) * shard + place % shard + me * group
    copies[0].wait()
    nodes = jnp.broadcast_to(order_ref[...][:, None, :], (colblk, width // colblk, width))
    nodes = nodes.reshape(width, width).T
    for k in range(colblk):
        column = nodes[:, k * (width // colblk):k * (width // colblk) + 1]
        pick_ref[k * width:(k + 1) * width, :] = jnp.where(corpus == column, 1.0, 0.0).astype(pick_ref.dtype)
    copies[1].wait()
    copies[2].wait()

    def step(index, carry):
        code = slots_ref[0, 0, index]
        columns = pl.ds(pl.multiple_of(lax.rem(code, colblk) * width, width), width)
        for part in range(width // piece):
            start = code // colblk * width + part * piece
            slot = (start // rows) ^ me
            at = place_of(slot, (me ^ slot) & 1, bits) * rows + lax.rem(start, rows)
            at = pl.ds(pl.multiple_of(at, piece), piece)
            values = blocks_ref[0, 0, index, part * piece:(part + 1) * piece, :]

            @pl.when(slot & 1 == 0)
            def _():
                keep_ref[at, columns] = values

            @pl.when(slot & 1 == 1)
            def _():
                give_ref[at, columns] = values

        return carry

    lax.fori_loop(0, count_ref[0, 0], step, 0)


def order_kernel(pick_ref, *refs):
    features, ordered_ref = refs[:-1], refs[-1]
    x = jnp.concatenate([ref[...] for ref in features], axis=0)
    ordered_ref[...] = jnp.dot(pick_ref[...], x, preferred_element_type=jnp.float32).astype(ordered_ref.dtype)


def sum_kernel(tile_ref, ordered_ref, out_ref):
    out_ref[...] = jnp.dot(tile_ref[...], ordered_ref[...], preferred_element_type=jnp.float32).astype(out_ref.dtype)


def add_kernel(mine_ref, got_ref, hold_ref, *sends):
    count = hold_ref.shape[0]
    hold_ref[...] = mine_ref[:count, :] + got_ref[:count, :].astype(jnp.float32)
    for send_ref in sends:
        here = slice(count, count + send_ref.shape[0])
        send_ref[...] = (mine_ref[here, :] + got_ref[here, :].astype(jnp.float32)).astype(send_ref.dtype)
        count += send_ref.shape[0]


def relay_kernel(mine_ref, got_ref, *sends):
    offset = got_ref.shape[0]
    start = 0
    for send_ref in sends:
        count = send_ref.shape[0]
        total = mine_ref[offset + start:offset + start + count, :] + got_ref[start:start + count, :].astype(jnp.float32)
        send_ref[...] = total.astype(send_ref.dtype)
        start += count


def keep_kernel(mine_ref, got_ref, hold_ref):
    hold_ref[...] = mine_ref[:hold_ref.shape[0], :] + got_ref[...].astype(jnp.float32)


def project_kernel(start, first, last, *refs):
    mine_ref, near_ref, far_ref, weight_ref = refs[:4]
    before, out_ref = refs[4:-1], refs[-1]
    total = mine_ref[:near_ref.shape[0], :] + near_ref[...].astype(jnp.float32) + far_ref[...].astype(jnp.float32)
    projected = jnp.dot(
        total.astype(jnp.bfloat16), weight_ref[start:start + total.shape[1], :], preferred_element_type=jnp.float32
    )
    if not first:
        projected += before[0][...]
    out_ref[...] = (jnp.maximum(projected, 0.0) if last else projected).astype(out_ref.dtype)


def per_device(features, order, tile_count, tile_slots, blocks, weight):
    rows_axis, cols_axis = lax.axis_size("row"), lax.axis_size("col")
    bits = cols_axis.bit_length() - 2
    half = cols_axis // 2
    shard, feats = features.shape
    group = shard * rows_axis
    width = blocks.shape[-1]
    rows = shard
    params = pltpu.CompilerParams(vmem_limit_bytes=VMEM_LIMIT)
    vmem = pl.BlockSpec(memory_space=pltpu.VMEM)
    smem = pl.BlockSpec(memory_space=pltpu.SMEM)
    hbm = pl.BlockSpec(memory_space=pltpu.HBM)
    bf16, f32 = jnp.bfloat16, jnp.float32
    shape = jax.ShapeDtypeStruct

    def call(kernel, outs, ins, specs=None, scratch=(), cost=COST):
        return pl.pallas_call(
            kernel,
            out_shape=outs,
            in_specs=specs or [vmem] * len(ins),
            out_specs=jax.tree.map(lambda _: vmem, outs),
            scratch_shapes=scratch,
            compiler_params=params,
            cost_estimate=pl.CostEstimate(flops=cost, bytes_accessed=cost, transcendentals=0),
        )(*ins)

    def in_hbm(x):
        return pltpu.with_memory_space_constraint(x, pltpu.HBM)

    def after(x, *done):
        return lax.optimization_barrier((x, *done))[0]

    def exchange(x, axis, distance):
        return lax.ppermute(x, axis, [(i, i ^ distance) for i in range(lax.axis_size(axis))])

    def exchange_chips(x, step):
        far = cols_axis >> (step + 1)
        near = 2 << step
        return lax.ppermute(x, "col", [(j, j ^ (far if j & 1 else near)) for j in range(cols_axis)])

    widths = [feats * share // sum(SHARES) for share in SHARES]
    cuts = call(
        cut_kernel, [shape((shard, depth), bf16) for depth in widths], [in_hbm(features)],
        [hbm], [pltpu.SemaphoreType.DMA((len(widths),))], 1,
    )
    table = (group // width, width)
    give, keep, pick = call(
        functools.partial(tile_kernel, bits, rows, shard),
        [shape((half * rows, group), bf16)] * 2 + [shape((group, group), bf16)],
        [in_hbm(order.reshape(table)), in_hbm(blocks), in_hbm(tile_slots), tile_count],
        [hbm, hbm, hbm, smem],
        [
            pltpu.VMEM(table, jnp.int32),
            pltpu.VMEM(blocks.shape, bf16),
            pltpu.SMEM(tile_slots.shape, jnp.int32),
            pltpu.SemaphoreType.DMA((3,)),
        ],
    )

    gathered = []
    for mine in cuts:
        mine = after(mine, give) if gathered else mine
        gathered.append([mine] + [exchange(mine, "row", k) for k in range(1, rows_axis)])

    def pieces(count, depth):
        return [shape((count // 2 * rows, depth), bf16)] * 2 if count > 1 else [shape((rows, depth), bf16)]

    def first_step(mine, got):
        depth = mine.shape[1]
        outs = [shape((half // 2 * rows, depth), f32)] + pieces(half // 2, depth)
        hold, low, high = call(add_kernel, outs, [mine, got])
        return hold, exchange_chips(high, 0), exchange_chips(low, 0)

    def later_steps(hold, high, low):
        step, depth = 1, hold.shape[1]
        while True:
            count = hold.shape[0] // (2 * rows)
            sends = call(relay_kernel, pieces(count, depth), [hold, high])
            sent[:] = sends
            if count == 1:
                return [hold, low, exchange_chips(sends[0], step)]
            hold = call(keep_kernel, shape((count * rows, depth), f32), [hold, low])
            low, high = [exchange_chips(send, step) for send in sends]
            step += 1

    ends, waiting, sent = [], None, []
    for features, depth in zip(gathered, widths, strict=True):
        if waiting is not None:
            features = [after(features[0], waiting[0]), *features[1:]]
        ordered = call(order_kernel, shape((group, depth), bf16), [pick, *features])
        given = call(sum_kernel, shape((half * rows, depth), bf16), [give, ordered])
        got = exchange(given, "col", 1)
        if waiting is not None:
            ends += later_steps(waiting[0], after(waiting[1], given), waiting[2])
            ordered = after(ordered, sent[0])
        mine = call(sum_kernel, shape((half * rows, depth), f32), [keep, ordered])
        waiting = first_step(mine, got)
    ends += later_steps(waiting[0], after(waiting[1], *ends[1::3], *ends[2::3]), waiting[2])
    projected, start = [], 0
    for k, depth in enumerate(widths):
        first, last = k == 0, k == len(widths) - 1
        terms = ends[3 * k:3 * k + 3]
        if not last:
            terms[0] = after(terms[0], sent[0])
        projected = [call(
            functools.partial(project_kernel, start, first, last), shape((rows, feats), bf16 if last else f32),
            [*terms, weight, *projected], cost=1,
        )]
        start += depth
    return projected[0]


def solution(mesh):
    in_specs = (
        P(("col", "row"), None),
        P("col"),
        P("row", "col"),
        P("row", "col", None),
        P("row", "col", None, None, None),
        P(),
    )
    out_specs = P(("row", "col"), None)
    return jax.shard_map(
        per_device, mesh=mesh, in_specs=in_specs, out_specs=out_specs, check_vma=False
    )
```

```python
import functools

import jax
import jax.numpy as jnp
from jax import lax
from jax.experimental import pallas as pl
from jax.experimental.pallas import tpu as pltpu
from jax.sharding import PartitionSpec as P

VMEM_LIMIT = 16 * 1024 * 1024
SHARES = (1, 1)
COST = 10**10
OUT_PIECES = 2


def cut_kernel(x_hbm, *refs):
    outs, sems = refs[:-1], refs[-1]
    copies, start = [], 0
    for k, out in enumerate(outs):
        depth = out.shape[1]
        copies.append(pltpu.make_async_copy(x_hbm.at[:, pl.ds(start, depth)], out, sems.at[k]))
        start += depth
    for copy in copies:
        copy.start()
    for copy in copies:
        copy.wait()


def place_of(slot, core, bits):
    near = 0
    for bit in range(bits):
        near += ((slot >> (bit + 1)) & 1) << (bits - 1 - bit)
    return jnp.where(core == 0, near, slot >> 1)


def tile_kernel(bits, rows, shard, order_hbm, blocks_hbm, slots_hbm, count_ref, give_ref, keep_ref, pick_ref,
                order_ref, blocks_ref, slots_ref, sems):
    copies = [
        pltpu.make_async_copy(src, dst, sems.at[k])
        for k, (src, dst) in enumerate(((order_hbm, order_ref), (blocks_hbm, blocks_ref), (slots_hbm, slots_ref)))
    ]
    for copy in copies:
        copy.start()
    group = keep_ref.shape[1]
    width = blocks_ref.shape[-1]
    colblk = group // width
    piece = min(rows, width)
    me = lax.axis_index("col")
    row = lax.axis_index("row")
    keep_ref[...] = jnp.zeros_like(keep_ref)
    give_ref[...] = jnp.zeros_like(give_ref)
    place = lax.broadcasted_iota(jnp.int32, (width, group), 1)
    corpus = ((place // shard) ^ row) * shard + place % shard + me * group
    copies[0].wait()
    nodes = jnp.broadcast_to(order_ref[...][:, None, :], (colblk, width // colblk, width))
    nodes = nodes.reshape(width, width).T
    for k in range(colblk):
        column = nodes[:, k * (width // colblk):k * (width // colblk) + 1]
        pick_ref[k * width:(k + 1) * width, :] = jnp.where(corpus == column, 1.0, 0.0).astype(pick_ref.dtype)
    copies[1].wait()
    copies[2].wait()

    def step(index, carry):
        code = slots_ref[0, 0, index]
        columns = pl.ds(pl.multiple_of(lax.rem(code, colblk) * width, width), width)
        for part in range(width // piece):
            start = code // colblk * width + part * piece
            slot = (start // rows) ^ me
            at = place_of(slot, (me ^ slot) & 1, bits) * rows + lax.rem(start, rows)
            at = pl.ds(pl.multiple_of(at, piece), piece)
            values = blocks_ref[0, 0, index, part * piece:(part + 1) * piece, :]

            @pl.when(slot & 1 == 0)
            def _():
                keep_ref[at, columns] = values

            @pl.when(slot & 1 == 1)
            def _():
                give_ref[at, columns] = values

        return carry

    lax.fori_loop(0, count_ref[0, 0], step, 0)


def order_kernel(pick_ref, *refs):
    features, ordered_ref = refs[:-1], refs[-1]
    x = jnp.concatenate([ref[...] for ref in features], axis=0)
    ordered_ref[...] = jnp.dot(pick_ref[...], x, preferred_element_type=jnp.float32).astype(ordered_ref.dtype)


def sum_kernel(tile_ref, ordered_ref, out_ref):
    out_ref[...] = jnp.dot(tile_ref[...], ordered_ref[...], preferred_element_type=jnp.float32).astype(out_ref.dtype)


def add_kernel(mine_ref, got_ref, hold_ref, *sends):
    count = hold_ref.shape[0]
    hold_ref[...] = mine_ref[:count, :] + got_ref[:count, :].astype(jnp.float32)
    for send_ref in sends:
        here = slice(count, count + send_ref.shape[0])
        send_ref[...] = (mine_ref[here, :] + got_ref[here, :].astype(jnp.float32)).astype(send_ref.dtype)
        count += send_ref.shape[0]


def relay_kernel(mine_ref, got_ref, *sends):
    offset = got_ref.shape[0]
    start = 0
    for send_ref in sends:
        count = send_ref.shape[0]
        total = mine_ref[offset + start:offset + start + count, :] + got_ref[start:start + count, :].astype(jnp.float32)
        send_ref[...] = total.astype(send_ref.dtype)
        start += count


def keep_kernel(mine_ref, got_ref, hold_ref):
    hold_ref[...] = mine_ref[:hold_ref.shape[0], :] + got_ref[...].astype(jnp.float32)


def project_kernel(start, first, last, *refs):
    mine_ref, near_ref, far_ref, weight_ref = refs[:4]
    before, out_ref = (refs[4:5], refs[5]) if not first else ((), refs[4])
    rows = far_ref.shape[0]
    weight = weight_ref[start:start + far_ref.shape[1], :]

    def some(here):
        total = mine_ref[here, :] + near_ref[here, :].astype(jnp.float32) + far_ref[here, :].astype(jnp.float32)
        projected = jnp.dot(total.astype(jnp.bfloat16), weight, preferred_element_type=jnp.float32)
        return projected if first else projected + before[0][here, :]

    if not last:
        out_ref[...] = some(slice(0, rows))
        return
    held_ref, sems = refs[-2], refs[-1]
    count = rows // OUT_PIECES
    copies = []
    for k in range(OUT_PIECES):
        here = slice(k * count, (k + 1) * count)
        held_ref[here, :] = jnp.maximum(some(here), 0.0).astype(held_ref.dtype)
        copies.append(pltpu.make_async_copy(
            held_ref.at[pl.ds(k * count, count), :], out_ref.at[pl.ds(k * count, count), :], sems.at[k]
        ))
        copies[-1].start()
    for copy in copies:
        copy.wait()


def per_device(features, order, tile_count, tile_slots, blocks, weight):
    rows_axis, cols_axis = lax.axis_size("row"), lax.axis_size("col")
    bits = cols_axis.bit_length() - 2
    half = cols_axis // 2
    shard, feats = features.shape
    group = shard * rows_axis
    width = blocks.shape[-1]
    rows = shard
    params = pltpu.CompilerParams(vmem_limit_bytes=VMEM_LIMIT)
    vmem = pl.BlockSpec(memory_space=pltpu.VMEM)
    smem = pl.BlockSpec(memory_space=pltpu.SMEM)
    hbm = pl.BlockSpec(memory_space=pltpu.HBM)
    bf16, f32 = jnp.bfloat16, jnp.float32
    shape = jax.ShapeDtypeStruct

    def call(kernel, outs, ins, specs=None, scratch=(), cost=COST, out_hbm=False):
        return pl.pallas_call(
            kernel,
            out_shape=outs,
            in_specs=specs or [vmem] * len(ins),
            out_specs=jax.tree.map(lambda _: hbm if out_hbm else vmem, outs),
            scratch_shapes=scratch,
            compiler_params=params,
            cost_estimate=pl.CostEstimate(flops=cost, bytes_accessed=cost, transcendentals=0),
        )(*ins)

    def in_hbm(x):
        return pltpu.with_memory_space_constraint(x, pltpu.HBM)

    def after(x, *done):
        return lax.optimization_barrier((x, *done))[0]

    def exchange(x, axis, distance):
        return lax.ppermute(x, axis, [(i, i ^ distance) for i in range(lax.axis_size(axis))])

    def exchange_chips(x, step):
        far = cols_axis >> (step + 1)
        near = 2 << step
        return lax.ppermute(x, "col", [(j, j ^ (far if j & 1 else near)) for j in range(cols_axis)])

    widths = [feats * share // sum(SHARES) for share in SHARES]
    cuts = call(
        cut_kernel, [shape((shard, depth), bf16) for depth in widths], [in_hbm(features)],
        [hbm], [pltpu.SemaphoreType.DMA((len(widths),))], 1,
    )
    table = (group // width, width)
    give, keep, pick = call(
        functools.partial(tile_kernel, bits, rows, shard),
        [shape((half * rows, group), bf16)] * 2 + [shape((group, group), bf16)],
        [in_hbm(order.reshape(table)), in_hbm(blocks), in_hbm(tile_slots), tile_count],
        [hbm, hbm, hbm, smem],
        [
            pltpu.VMEM(table, jnp.int32),
            pltpu.VMEM(blocks.shape, bf16),
            pltpu.SMEM(tile_slots.shape, jnp.int32),
            pltpu.SemaphoreType.DMA((3,)),
        ],
    )

    gathered = []
    for mine in cuts:
        mine = after(mine, give) if gathered else mine
        gathered.append([mine] + [exchange(mine, "row", k) for k in range(1, rows_axis)])

    def pieces(count, depth):
        return [shape((count // 2 * rows, depth), bf16)] * 2 if count > 1 else [shape((rows, depth), bf16)]

    def first_step(mine, got):
        depth = mine.shape[1]
        outs = [shape((half // 2 * rows, depth), f32)] + pieces(half // 2, depth)
        hold, low, high = call(add_kernel, outs, [mine, got])
        return hold, exchange_chips(high, 0), exchange_chips(low, 0)

    def later_steps(hold, high, low):
        step, depth = 1, hold.shape[1]
        while True:
            count = hold.shape[0] // (2 * rows)
            sends = call(relay_kernel, pieces(count, depth), [hold, high])
            sent[:] = sends
            if count == 1:
                return [hold, low, exchange_chips(sends[0], step)]
            hold = call(keep_kernel, shape((count * rows, depth), f32), [hold, low])
            low, high = [exchange_chips(send, step) for send in sends]
            step += 1

    ends, waiting, sent = [], None, []
    for features, depth in zip(gathered, widths, strict=True):
        if waiting is not None:
            features = [after(features[0], waiting[0]), *features[1:]]
        ordered = call(order_kernel, shape((group, depth), bf16), [pick, *features])
        given = call(sum_kernel, shape((half * rows, depth), bf16), [give, ordered])
        got = exchange(given, "col", 1)
        if waiting is not None:
            ends += later_steps(waiting[0], after(waiting[1], given), waiting[2])
            ordered = after(ordered, sent[0])
        mine = call(sum_kernel, shape((half * rows, depth), f32), [keep, ordered])
        waiting = first_step(mine, got)
    ends += later_steps(waiting[0], after(waiting[1], *ends[1::3], *ends[2::3]), waiting[2])
    projected, start = [], 0
    for k, depth in enumerate(widths):
        first, last = k == 0, k == len(widths) - 1
        terms = ends[3 * k:3 * k + 3]
        if not last:
            terms[0] = after(terms[0], sent[0])
        projected = [call(
            functools.partial(project_kernel, start, first, last), shape((rows, feats), bf16 if last else f32),
            [*terms, weight, *projected], cost=1, out_hbm=last,
            scratch=[pltpu.VMEM((rows, feats), bf16), pltpu.SemaphoreType.DMA((OUT_PIECES,))] if last else (),
        )]
        start += depth
    return projected[0]


def solution(mesh):
    in_specs = (
        P(("col", "row"), None),
        P("col"),
        P("row", "col"),
        P("row", "col", None),
        P("row", "col", None, None, None),
        P(),
    )
    out_specs = P(("row", "col"), None)
    return jax.shard_map(
        per_device, mesh=mesh, in_specs=in_specs, out_specs=out_specs, check_vma=False
    )
```

```python
import functools

import jax
import jax.numpy as jnp
from jax import lax
from jax.experimental import pallas as pl
from jax.experimental.pallas import tpu as pltpu
from jax.sharding import PartitionSpec as P

VMEM_LIMIT = 16 * 1024 * 1024
SHARES = (1, 1)
COST = 10**10


def cut_kernel(start, x_hbm, out_ref, sem):
    copy = pltpu.make_async_copy(x_hbm.at[:, pl.ds(start, out_ref.shape[1])], out_ref, sem)
    copy.start()
    copy.wait()


def place_of(slot, core, bits):
    near = 0
    for bit in range(bits):
        near += ((slot >> (bit + 1)) & 1) << (bits - 1 - bit)
    return jnp.where(core == 0, near, slot >> 1)


def tile_kernel(bits, rows, shard, order_hbm, blocks_hbm, slots_hbm, x_hbm, count_ref, give_ref, keep_ref, pick_ref,
                cut_ref, order_ref, blocks_ref, slots_ref, sems):
    copies = [
        pltpu.make_async_copy(src, dst, sems.at[k])
        for k, (src, dst) in enumerate(((order_hbm, order_ref), (blocks_hbm, blocks_ref), (slots_hbm, slots_ref), (
            x_hbm.at[:, pl.ds(x_hbm.shape[1] - cut_ref.shape[1], cut_ref.shape[1])], cut_ref,
        )))
    ]
    for copy in copies:
        copy.start()
    group = keep_ref.shape[1]
    width = blocks_ref.shape[-1]
    colblk = group // width
    piece = min(rows, width)
    me = lax.axis_index("col")
    row = lax.axis_index("row")
    keep_ref[...] = jnp.zeros_like(keep_ref)
    give_ref[...] = jnp.zeros_like(give_ref)
    place = lax.broadcasted_iota(jnp.int32, (width, group), 1)
    corpus = ((place // shard) ^ row) * shard + place % shard + me * group
    copies[0].wait()
    nodes = jnp.broadcast_to(order_ref[...][:, None, :], (colblk, width // colblk, width))
    nodes = nodes.reshape(width, width).T
    for k in range(colblk):
        column = nodes[:, k * (width // colblk):k * (width // colblk) + 1]
        pick_ref[k * width:(k + 1) * width, :] = jnp.where(corpus == column, 1.0, 0.0).astype(pick_ref.dtype)
    copies[1].wait()
    copies[2].wait()
    copies[3].wait()

    def step(index, carry):
        code = slots_ref[0, 0, index]
        columns = pl.ds(pl.multiple_of(lax.rem(code, colblk) * width, width), width)
        for part in range(width // piece):
            start = code // colblk * width + part * piece
            slot = (start // rows) ^ me
            at = place_of(slot, (me ^ slot) & 1, bits) * rows + lax.rem(start, rows)
            at = pl.ds(pl.multiple_of(at, piece), piece)
            values = blocks_ref[0, 0, index, part * piece:(part + 1) * piece, :]

            @pl.when(slot & 1 == 0)
            def _():
                keep_ref[at, columns] = values

            @pl.when(slot & 1 == 1)
            def _():
                give_ref[at, columns] = values

        return carry

    lax.fori_loop(0, count_ref[0, 0], step, 0)


def order_kernel(pick_ref, *refs):
    features, ordered_ref = refs[:-1], refs[-1]
    x = jnp.concatenate([ref[...] for ref in features], axis=0)
    ordered_ref[...] = jnp.dot(pick_ref[...], x, preferred_element_type=jnp.float32).astype(ordered_ref.dtype)


def sum_kernel(tile_ref, ordered_ref, out_ref):
    out_ref[...] = jnp.dot(tile_ref[...], ordered_ref[...], preferred_element_type=jnp.float32).astype(out_ref.dtype)


def add_kernel(mine_ref, got_ref, hold_ref, *sends):
    count = hold_ref.shape[0]
    hold_ref[...] = mine_ref[:count, :] + got_ref[:count, :].astype(jnp.float32)
    for send_ref in sends:
        here = slice(count, count + send_ref.shape[0])
        send_ref[...] = (mine_ref[here, :] + got_ref[here, :].astype(jnp.float32)).astype(send_ref.dtype)
        count += send_ref.shape[0]


def relay_kernel(mine_ref, got_ref, *sends):
    offset = got_ref.shape[0]
    start = 0
    for send_ref in sends:
        count = send_ref.shape[0]
        total = mine_ref[offset + start:offset + start + count, :] + got_ref[start:start + count, :].astype(jnp.float32)
        send_ref[...] = total.astype(send_ref.dtype)
        start += count


def keep_kernel(mine_ref, got_ref, hold_ref):
    hold_ref[...] = mine_ref[:hold_ref.shape[0], :] + got_ref[...].astype(jnp.float32)


def project_kernel(start, first, last, *refs):
    mine_ref, near_ref, far_ref, weight_ref = refs[:4]
    before, out_ref = refs[4:-1], refs[-1]
    total = mine_ref[:near_ref.shape[0], :] + near_ref[...].astype(jnp.float32) + far_ref[...].astype(jnp.float32)
    projected = jnp.dot(
        total.astype(jnp.bfloat16), weight_ref[start:start + total.shape[1], :], preferred_element_type=jnp.float32
    )
    if not first:
        projected += before[0][...]
    out_ref[...] = (jnp.maximum(projected, 0.0) if last else projected).astype(out_ref.dtype)


def per_device(features, order, tile_count, tile_slots, blocks, weight):
    rows_axis, cols_axis = lax.axis_size("row"), lax.axis_size("col")
    bits = cols_axis.bit_length() - 2
    half = cols_axis // 2
    shard, feats = features.shape
    group = shard * rows_axis
    width = blocks.shape[-1]
    rows = shard
    params = pltpu.CompilerParams(vmem_limit_bytes=VMEM_LIMIT)
    vmem = pl.BlockSpec(memory_space=pltpu.VMEM)
    smem = pl.BlockSpec(memory_space=pltpu.SMEM)
    hbm = pl.BlockSpec(memory_space=pltpu.HBM)
    bf16, f32 = jnp.bfloat16, jnp.float32
    shape = jax.ShapeDtypeStruct

    def call(kernel, outs, ins, specs=None, scratch=(), cost=COST):
        return pl.pallas_call(
            kernel,
            out_shape=outs,
            in_specs=specs or [vmem] * len(ins),
            out_specs=jax.tree.map(lambda _: vmem, outs),
            scratch_shapes=scratch,
            compiler_params=params,
            cost_estimate=pl.CostEstimate(flops=cost, bytes_accessed=cost, transcendentals=0),
        )(*ins)

    def in_hbm(x):
        return pltpu.with_memory_space_constraint(x, pltpu.HBM)

    def after(x, *done):
        return lax.optimization_barrier((x, *done))[0]

    def exchange(x, axis, distance):
        return lax.ppermute(x, axis, [(i, i ^ distance) for i in range(lax.axis_size(axis))])

    def exchange_chips(x, step):
        far = cols_axis >> (step + 1)
        near = 2 << step
        return lax.ppermute(x, "col", [(j, j ^ (far if j & 1 else near)) for j in range(cols_axis)])

    widths = [feats * share // sum(SHARES) for share in SHARES]
    cuts, start = [], 0
    for depth in widths[:-1]:
        cuts.append(call(
            functools.partial(cut_kernel, start), shape((shard, depth), bf16), [in_hbm(features)],
            [hbm], [pltpu.SemaphoreType.DMA], 1,
        ))
        start += depth
    table = (group // width, width)
    give, keep, pick, cut = call(
        functools.partial(tile_kernel, bits, rows, shard),
        [shape((half * rows, group), bf16)] * 2
        + [shape((group, group), bf16), shape((shard, widths[-1]), bf16)],
        [in_hbm(order.reshape(table)), in_hbm(blocks), in_hbm(tile_slots), in_hbm(features), tile_count],
        [hbm, hbm, hbm, hbm, smem],
        [
            pltpu.VMEM(table, jnp.int32),
            pltpu.VMEM(blocks.shape, bf16),
            pltpu.SMEM(tile_slots.shape, jnp.int32),
            pltpu.SemaphoreType.DMA((4,)),
        ],
    )
    cuts.append(cut)

    gathered = []
    for mine in cuts:
        mine = after(mine, give) if gathered else mine
        gathered.append([mine] + [exchange(mine, "row", k) for k in range(1, rows_axis)])

    def pieces(count, depth):
        return [shape((count // 2 * rows, depth), bf16)] * 2 if count > 1 else [shape((rows, depth), bf16)]

    def first_step(mine, got):
        depth = mine.shape[1]
        outs = [shape((half // 2 * rows, depth), f32)] + pieces(half // 2, depth)
        hold, low, high = call(add_kernel, outs, [mine, got])
        return hold, exchange_chips(high, 0), exchange_chips(low, 0)

    def later_steps(hold, high, low):
        step, depth = 1, hold.shape[1]
        while True:
            count = hold.shape[0] // (2 * rows)
            sends = call(relay_kernel, pieces(count, depth), [hold, high])
            sent[:] = sends
            if count == 1:
                return [hold, low, exchange_chips(sends[0], step)]
            hold = call(keep_kernel, shape((count * rows, depth), f32), [hold, low])
            low, high = [exchange_chips(send, step) for send in sends]
            step += 1

    ends, waiting, sent = [], None, []
    for features, depth in zip(gathered, widths, strict=True):
        if waiting is not None:
            features = [after(features[0], waiting[0]), *features[1:]]
        ordered = call(order_kernel, shape((group, depth), bf16), [pick, *features])
        given = call(sum_kernel, shape((half * rows, depth), bf16), [give, ordered])
        got = exchange(given, "col", 1)
        if waiting is not None:
            ends += later_steps(waiting[0], after(waiting[1], given), waiting[2])
            ordered = after(ordered, sent[0])
        mine = call(sum_kernel, shape((half * rows, depth), f32), [keep, ordered])
        waiting = first_step(mine, got)
    ends += later_steps(waiting[0], after(waiting[1], *ends[1::3], *ends[2::3]), waiting[2])
    projected, start = [], 0
    for k, depth in enumerate(widths):
        first, last = k == 0, k == len(widths) - 1
        terms = ends[3 * k:3 * k + 3]
        if not last:
            terms[0] = after(terms[0], sent[0])
        projected = [call(
            functools.partial(project_kernel, start, first, last), shape((rows, feats), bf16 if last else f32),
            [*terms, weight, *projected], cost=1,
        )]
        start += depth
    return projected[0]


def solution(mesh):
    in_specs = (
        P(("col", "row"), None),
        P("col"),
        P("row", "col"),
        P("row", "col", None),
        P("row", "col", None, None, None),
        P(),
    )
    out_specs = P(("row", "col"), None)
    return jax.shard_map(
        per_device, mesh=mesh, in_specs=in_specs, out_specs=out_specs, check_vma=False
    )
```
